32 devices in a mesh: row: 8 (over y, x, core), col: 4 (over z).
Axes of the slice: x: 2, y: 2, z: 4, core: 2. Of those that a mesh axis runs over, the one named last changes fastest.
Arguments:
- stored_blocks: bfloat16 [8, 4, 64, 128, 128], P('row', 'col'), may hold values from -1 to 1
- stored_ids: int32 [8, 4, 3, 64], P('row', 'col'), may hold values from 0 to 127, as said below
- slab_blocks: bfloat16 [8, 4, 32, 128, 128], P('row', 'col'), may hold values from -1 to 1
- slab_ids: int32 [8, 4, 3, 32], P('row', 'col'), may hold values from 0 to 127, as said below
- pair_lists: int32 [8, 4, 4, 3, 256], P('row', 'col'), may hold values from 0 to 127, as said below
Outputs:
- product: bfloat16 [16384, 1024], P('row', 'col')
The draws below stay inside these ranges and needn't reach their ends.
Inputs may be any that keep to these rules, and one draw needn't show every extreme that they name: `stored_ids`: present slots of cell (r, c) hold blocks of the panel pair made of panels r and r xor c: row index in the lower of the two panels (panel p covers block rows p * 16 to (p + 1) * 16 - 1), column index in the higher, row <= column. Every stored block lies in exactly one slot over all cells. Flags are 0 or 1; a half has at most 64 present slots and some halves have exactly 64. `slab_ids`: the slots of cell (r, c) name each block of panel r xor c and slab columns c * 2 to (c + 1) * 2 - 1 exactly once; flags are 0 or 1, and some cells have all flags 1. pair_lists[r, c, s] names, with flag 1 and ahead of every entry with flag 0, each pair of a present entry of A_s and a present entry of B_s whose column index and row index agree, once each; some list has all 256 flags 1.
All inputs are finite; a program needn't handle non-finite values.
Results may differ from the reference program's by a relative error of at most 0.001.
Values may be sent and summed in bfloat16 or wider, within the bound.
A program may use at most 128 MiB of HBM per device.

```python
import jax
import jax.numpy as jnp
from jax import lax

BLOCK = 128
PANEL = 16
SLAB = 2
STEPS = 4
HALF = 64
SLAB_SLOTS = 32
PAIRS = 256
N_ROW = 8
N_COL = 4


def orient_ids(block_ids, transpose, drop_diag):
    col_ids = jnp.where(transpose, block_ids[0], block_ids[1])
    present = block_ids[2]
    if drop_diag:
        present = present * (block_ids[0] != block_ids[1]).astype(jnp.int32)
    return (col_ids, present)


def layout(key):
    tile_size = PANEL * PANEL
    grid_rows = jnp.arange(N_ROW, dtype=jnp.int32)
    grid_cols = jnp.arange(N_COL, dtype=jnp.int32)

    def stored_half(grid_row, grid_col):
        panel_index = jnp.bitwise_xor(grid_row, grid_col)
        lower = jnp.minimum(grid_row, panel_index)
        upper = jnp.maximum(grid_row, panel_index)
        tile_key = jax.random.fold_in(jax.random.fold_in(key, 11), lower * N_ROW + upper)
        level = jax.random.randint(jax.random.fold_in(tile_key, 1), (), 0, 4)
        lowered = jnp.where(level == 0, 0, jnp.where(level == 3, 2, 1))
        lowered = jnp.where(lower == 0, 0, lowered)
        count = jnp.right_shift(jnp.int32(HALF), lowered.astype(jnp.int32))
        places = jnp.arange(tile_size, dtype=jnp.int32)
        local_row = places // PANEL
        local_col = places % PANEL
        eligible = jnp.where(lower == upper, local_row <= local_col, True)
        ranking = jax.random.permutation(jax.random.fold_in(tile_key, 2), tile_size).astype(jnp.int32)
        scores = jnp.where(eligible, tile_size, 0).astype(jnp.int32) + ranking
        ordered = jnp.argsort(-scores, stable=True).astype(jnp.int32)
        start = jnp.where((grid_row == upper) & (lower != upper), count, 0)
        picks = jnp.take(ordered, start + jnp.arange(HALF, dtype=jnp.int32))
        present = (jnp.arange(HALF, dtype=jnp.int32) < count).astype(jnp.int32)
        device_key = jax.random.fold_in(jax.random.fold_in(key, 13), grid_row * N_COL + grid_col)
        slot_order = jax.random.permutation(device_key, HALF)
        picks = picks[slot_order]
        present = present[slot_order]
        global_row = lower * PANEL + picks // PANEL
        global_col = upper * PANEL + picks % PANEL
        return jnp.stack([global_row, global_col, present]).astype(jnp.int32)
    stored_ids = jax.vmap(jax.vmap(stored_half, (None, 0)), (0, None))(grid_rows, grid_cols)

    def slab_tile(grid_row, grid_col):
        panel_index = jnp.bitwise_xor(grid_row, grid_col)
        device_key = jax.random.fold_in(jax.random.fold_in(key, 17), grid_row * N_COL + grid_col)
        places = jnp.arange(SLAB_SLOTS, dtype=jnp.int32)
        keeping = jax.random.randint(jax.random.fold_in(device_key, 1), (SLAB_SLOTS,), 0, 4) > 0
        keeping = keeping | (grid_row == 0)
        slot_order = jax.random.permutation(jax.random.fold_in(device_key, 2), SLAB_SLOTS)
        places = places[slot_order]
        keeping = keeping[slot_order]
        global_row = panel_index * PANEL + places // SLAB
        global_col = grid_col * SLAB + places % SLAB
        return jnp.stack([global_row, global_col, keeping.astype(jnp.int32)]).astype(jnp.int32)
    slab_ids = jax.vmap(jax.vmap(slab_tile, (None, 0)), (0, None))(grid_rows, grid_cols)
    candidates = 2 * HALF * SLAB_SLOTS
    stride_len = N_COL // STEPS

    def pair_list(grid_row, grid_col, offset):
        moved = offset * stride_len
        source = jnp.bitwise_xor(grid_col, moved)
        panel_index = jnp.bitwise_xor(grid_row, source)
        first_cols, first_present = orient_ids(stored_ids[grid_row, source], grid_row > panel_index, False)
        second_cols, second_present = orient_ids(stored_ids[panel_index, source], grid_row >= panel_index, True)
        left_cols = jnp.concatenate([first_cols, second_cols], 0)
        left_present = jnp.concatenate([first_present, second_present], 0)
        right_ids = slab_ids[jnp.bitwise_xor(grid_row, moved), grid_col]
        matching = (left_present[:, None] > 0) & (right_ids[2][None, :] > 0) & (left_cols[:, None] == right_ids[0][None, :])
        flat_match = matching.reshape(-1).astype(jnp.int32)
        list_key = jax.random.fold_in(jax.random.fold_in(key, 19), (grid_row * N_COL + grid_col) * STEPS + offset)
        breaking = jax.random.permutation(list_key, candidates).astype(jnp.int32)
        ordered = jnp.argsort(-(flat_match * candidates + breaking), stable=True).astype(jnp.int32)[:PAIRS]
        return jnp.stack([ordered // SLAB_SLOTS, ordered % SLAB_SLOTS, flat_match[ordered]]).astype(jnp.int32)
    offsets = jnp.arange(STEPS, dtype=jnp.int32)
    pair_lists = jax.vmap(jax.vmap(jax.vmap(pair_list, (None, None, 0)), (None, 0, None)), (0, None, None))(grid_rows, grid_cols, offsets)
    return (stored_ids, slab_ids, pair_lists)


def draw_stored_ids(key, part):
    return layout(key)[0]


def draw_slab_ids(key, part):
    return layout(key)[1]


def draw_pair_lists(key, part):
    return layout(key)[2]


def levels(stream_key, shape, split, smallest, high):
    factor_of = 1.0
    for position, blocks in split:
        steps = jax.random.uniform(jax.random.fold_in(jax.random.fold_in(stream_key, 6), position), (blocks,), jnp.float32, smallest / len(split), high / len(split))
        factor_of = factor_of * jnp.repeat(jnp.exp(steps), shape[position] // blocks).reshape((-1,) + (1,) * (len(shape) - 1 - position))
    return factor_of


def normal_values(own_key, shape, scale, bound, pieces=(), held_as=jnp.bfloat16):
    entries = jax.random.normal(own_key, shape, jnp.float32) * scale
    if len(pieces) > 0:
        entries = levels(own_key, shape, pieces, -0.22, 0.18) * entries
    return jnp.clip(entries, min=-bound, max=bound).astype(held_as)


def setup_inputs(seed: int = 0) -> dict:
    streams_of = jax.random.split(jax.random.key(seed), 6)
    stored_blocks = normal_values(streams_of[0], (N_ROW, N_COL, HALF, BLOCK, BLOCK), 0.16, 1.0, ((0, 8), (1, 4)))
    stored_ids = draw_stored_ids(jax.random.fold_in(streams_of[5], 71), 0)
    slab_blocks = normal_values(streams_of[2], (N_ROW, N_COL, SLAB_SLOTS, BLOCK, BLOCK), 0.16, 1.0, ((0, 8), (1, 4)))
    slab_ids = draw_slab_ids(jax.random.fold_in(streams_of[5], 71), 0)
    pair_lists = draw_pair_lists(jax.random.fold_in(streams_of[5], 71), 0)
    return dict(stored_blocks=stored_blocks, stored_ids=stored_ids, slab_blocks=slab_blocks, slab_ids=slab_ids, pair_lists=pair_lists)


def orient(values, block_ids, transpose, drop_diag):
    turned = jnp.where(transpose, jnp.swapaxes(values, 1, 2), values)
    row_ids = jnp.where(transpose, block_ids[1], block_ids[0])
    present = block_ids[2]
    if drop_diag:
        present = present * (block_ids[0] != block_ids[1]).astype(jnp.int32)
    return turned, row_ids, present


def reference(stored_blocks, stored_ids, slab_blocks, slab_ids, pair_lists):
    cell_count = PANEL * SLAB
    stride_len = N_COL // STEPS

    def one_device(device):
        grid_row = device // N_COL
        grid_col = device % N_COL
        summed = jnp.zeros((cell_count, BLOCK, BLOCK), jnp.float32)
        for offset in range(STEPS):
            moved = offset * stride_len
            source = jnp.bitwise_xor(grid_col, moved)
            panel_index = jnp.bitwise_xor(grid_row, source)
            first_blocks, first_rows, first_present = orient(
                stored_blocks[grid_row, source], stored_ids[grid_row, source], grid_row > panel_index, False)
            second_blocks, second_rows, second_present = orient(
                stored_blocks[panel_index, source], stored_ids[panel_index, source], grid_row >= panel_index, True)
            left_all = jnp.concatenate([first_blocks, second_blocks], 0)
            left_rows = jnp.concatenate([first_rows, second_rows], 0)
            left_present = jnp.concatenate([first_present, second_present], 0)
            slab_row = jnp.bitwise_xor(grid_row, moved)
            right_all = slab_blocks[slab_row, grid_col]
            right_ids = slab_ids[slab_row, grid_col]
            listed = pair_lists[grid_row, grid_col, offset]
            left_slot = listed[0]
            right_slot = listed[1]
            weights = listed[2] * left_present[left_slot] * right_ids[2][right_slot]
            target = (left_rows[left_slot] - grid_row * PANEL) * SLAB + right_ids[1][right_slot] - grid_col * SLAB
            target = jnp.where(weights > 0, target, cell_count).astype(jnp.int32)
            left_blocks = left_all[left_slot].astype(jnp.float32)
            right_blocks = right_all[right_slot].astype(jnp.float32)
            blocks = jnp.einsum("pij,pjk->pik", left_blocks, right_blocks)
            summed = summed + jax.ops.segment_sum(blocks, target, num_segments=cell_count + 1)[:cell_count]
        out_tile = summed.reshape(PANEL, SLAB, BLOCK, BLOCK).transpose(0, 2, 1, 3)
        return out_tile.reshape(PANEL * BLOCK, SLAB * BLOCK).astype(jnp.bfloat16)

    tiles = lax.map(one_device, jnp.arange(N_ROW * N_COL, dtype=jnp.int32))
    tiles = tiles.reshape(N_ROW, N_COL, PANEL * BLOCK, SLAB * BLOCK).transpose(0, 2, 1, 3)
    return tiles.reshape(N_ROW * PANEL * BLOCK, N_COL * SLAB * BLOCK)
```

```python
import functools

import jax
import jax.numpy as jnp
from jax import lax
from jax.experimental import pallas as pl
from jax.experimental.pallas import tpu as pltpu
from jax.sharding import PartitionSpec as P

PANEL = 16
SLAB = 2
STEPS = 4
CHUNKS = 4
MESH = pl.DeviceIdType.MESH


def flipped(value, mask, bits):
    out = value
    for b in range(bits):
        w = 2**b
        out = out + ((mask // w) % 2) * (w - 2 * w * ((value // w) % 2))
    return out


def gather_kernel(
    stride, bits, own, slab, ids, row_all, pair_all, slab_all, row_ids, pair_ids, slab_ids,
    z_send, z_recv, p_send, p_recv, b_send, b_recv, l_sem,
):
    r = lax.axis_index("row")
    c = lax.axis_index("col")
    pos = c // stride
    rem = c % stride
    left = c - stride
    right = c + stride
    size = own.shape[0] // CHUNKS

    def partner(s):
        return flipped(r, s * stride + rem, bits)

    def shifted(t):
        return flipped(r, t * stride, bits)

    bar = pltpu.get_barrier_semaphore()

    def greet(row, col):
        pl.semaphore_signal(bar, inc=1, device_id=(row, col), device_id_type=MESH)

    def cond_kind(s):
        return s * stride + rem > 0

    @pl.when(pos > 0)
    def _():
        greet(r, left)

    @pl.when(pos < STEPS - 1)
    def _():
        greet(r, right)

    for s in range(STEPS):
        @pl.when(cond_kind(s))
        def _():
            greet(partner(s), c)
    for t in range(1, STEPS):
        greet(shifted(t), c)

    ends = jnp.minimum(pos, 1) + jnp.minimum(STEPS - 1 - pos, 1)
    pl.semaphore_wait(bar, ends + jnp.minimum(rem, 1) + 2 * (STEPS - 1))

    def piece(ref, id_ref, ch):
        return id_ref if ch == 0 else ref.at[pl.ds((ch - 1) * size, size)]

    def landed(s, ch):
        return row_ids.at[s] if ch == 0 else row_all.at[s, pl.ds((ch - 1) * size, size)]

    def paired(s, ch):
        return pair_ids.at[s] if ch == 0 else pair_all.at[s, pl.ds((ch - 1) * size, size)]

    def along(src, s, ch, way):
        return pltpu.make_async_remote_copy(
            src_ref=src, dst_ref=landed(s, ch), send_sem=z_send.at[way, s, ch],
            recv_sem=z_recv.at[s, ch], device_id=(r, right if way else left), device_id_type=MESH)

    def across(src, s, ch):
        return pltpu.make_async_remote_copy(
            src_ref=src, dst_ref=paired(s, ch), send_sem=p_send.at[s, ch],
            recv_sem=p_recv.at[s, ch], device_id=(partner(s), c), device_id_type=MESH)

    def slab_copy(src, t, to, what):
        dst = slab_ids.at[t] if what == 0 else slab_all.at[t]
        return pltpu.make_async_remote_copy(
            src_ref=src, dst_ref=dst, send_sem=b_send.at[t, what],
            recv_sem=b_recv.at[t, what], device_id=(shifted(to), c), device_id_type=MESH)

    pieces = range(CHUNKS + 1)
    for ch in pieces:
        mine = piece(own, ids, ch)

        @pl.when(pos > 0)
        def _():
            along(mine, pos, ch, 0).start()

        @pl.when(pos < STEPS - 1)
        def _():
            along(mine, pos, ch, 1).start()

        @pl.when(cond_kind(pos))
        def _():
            across(mine, pos, ch).start()
        if ch == 0:
            for what, src in ((0, ids), (1, slab)):
                slab_copy(src, 2, 2, what).start()
                slab_copy(src, 1, 1, what).start()
    local = (
        pltpu.make_async_copy(own, row_all.at[pos], l_sem.at[0]),
        pltpu.make_async_copy(ids, row_ids.at[pos], l_sem.at[1]),
        pltpu.make_async_copy(slab, slab_all.at[0], l_sem.at[2]),
        pltpu.make_async_copy(ids, slab_ids.at[0], l_sem.at[3]),
    )
    for copy in local:
        copy.start()

    for d in range(1, STEPS):
        for ch in pieces:
            for way in (1, 0):
                s = pos - d if way else pos + d
                here = s >= 0 if way else s <= STEPS - 1
                more = pos < STEPS - 1 if way else pos > 0

                @pl.when(here)
                def _():
                    along(landed(s, ch), s, ch, way).wait_recv()

                    @pl.when(more)
                    def _():
                        along(landed(s, ch), s, ch, way).start()

                    @pl.when(cond_kind(s))
                    def _():
                        across(landed(s, ch), s, ch).start()
            if d == 1 and ch == 1:
                for what, src in ((0, slab_ids.at[2]), (1, slab_all.at[2])):
                    slab_copy(src, 2, 2, what).wait_recv()
                    slab_copy(src, 3, 1, what).start()

    for what, src in ((0, ids), (1, slab)):
        slab_copy(src, 1, 1, what).wait()
        slab_copy(src, 2, 2, what).wait_send()
        slab_copy(src, 3, 1, what).wait()
    for s in range(STEPS):
        for ch in pieces:
            @pl.when(cond_kind(s))
            def _():
                across(landed(s, ch), s, ch).wait()

            @pl.when(jnp.logical_and(s <= pos, pos < STEPS - 1))
            def _():
                along(landed(s, ch), s, ch, 1).wait_send()

            @pl.when(jnp.logical_and(s >= pos, pos > 0))
            def _():
                along(landed(s, ch), s, ch, 0).wait_send()
    for copy in local:
        copy.wait()


def gather(own, slab, ids, stride, bits):
    any_spec = pl.BlockSpec(memory_space=pl.ANY)
    dma = pltpu.SemaphoreType.DMA
    return pl.pallas_call(
        functools.partial(gather_kernel, stride, bits),
        out_shape=(
            jax.ShapeDtypeStruct((STEPS,) + own.shape, own.dtype),
            jax.ShapeDtypeStruct((STEPS,) + own.shape, own.dtype),
            jax.ShapeDtypeStruct((STEPS,) + slab.shape, slab.dtype),
            jax.ShapeDtypeStruct((STEPS,) + ids.shape, ids.dtype),
            jax.ShapeDtypeStruct((STEPS,) + ids.shape, ids.dtype),
            jax.ShapeDtypeStruct((STEPS,) + ids.shape, ids.dtype),
        ),
        in_specs=[any_spec] * 3,
        out_specs=(any_spec,) * 6,
        scratch_shapes=[
            dma((2, STEPS, CHUNKS + 1)), dma((STEPS, CHUNKS + 1)),
            dma((STEPS, CHUNKS + 1)), dma((STEPS, CHUNKS + 1)),
            dma((STEPS, 2)), dma((STEPS, 2)), dma((4,)),
        ],
        compiler_params=pltpu.CompilerParams(collective_id=0, has_side_effects=True),
    )(own, slab, ids)


def product_kernel(info, row_ids, pair_ids, slab_ids, row_ref, pair_ref, slab_ref, out, dense, right, acc):
    step = pl.program_id(0)
    r, q_mask, c = info[0], info[4 + step], info[1]
    slab_at = info[8 + step]
    q = r ^ q_mask
    slots, edge = row_ref.shape[1], row_ref.shape[2]
    low = jnp.minimum(r, q) * PANEL
    high = jnp.maximum(r, q) * PANEL

    @pl.when(step == 0)
    def _():
        acc[...] = jnp.zeros_like(acc)

    dense[...] = jnp.zeros_like(dense)
    right[...] = jnp.zeros_like(right)

    def put_slab(h, carry):
        k = slab_ids[slab_at, 3, h] - q * PANEL
        k = jnp.where(slab_ids[slab_at, 5, h] > 0, k, PANEL)
        n = slab_ids[slab_at, 4, h] - c * SLAB
        n = jnp.where(slab_ids[slab_at, 5, h] > 0, n, 0)
        lane = pl.multiple_of(n * edge, edge)
        right[k, :, pl.ds(lane, edge)] = slab_ref[0, h]
        return carry

    lax.fori_loop(0, slab_ref.shape[1], put_slab, 0, unroll=4)

    def put(ids, ref, turn, drop):
        def body(h, carry):
            i = ids[step, 0, h] - low
            j = ids[step, 1, h] - high
            keep = ids[step, 2, h] > 0
            if drop:
                keep = jnp.logical_and(keep, i != j)
            at_row, at_col = (j, i) if turn else (i, j)
            at_row = jnp.where(keep, at_row, PANEL)
            at_col = jnp.where(keep, at_col, 0)
            lane = pl.multiple_of(at_col * edge, edge)
            block = ref[0, h]
            dense[at_row, :, pl.ds(lane, edge)] = block.T if turn else block
            return carry

        lax.fori_loop(0, slots, body, 0, unroll=4)

    @pl.when(r < q)
    def _():
        put(row_ids, row_ref, False, False)
        put(pair_ids, pair_ref, False, False)

    @pl.when(r > q)
    def _():
        put(row_ids, row_ref, True, False)
        put(pair_ids, pair_ref, True, False)

    @pl.when(r == q)
    def _():
        put(row_ids, row_ref, False, False)
        put(row_ids, row_ref, True, True)

    depth = PANEL * edge
    group = 2
    slab_full = right[:PANEL].reshape(depth, SLAB * edge)

    def rows(g, carry):
        lhs = dense[pl.ds(g * group, group)].reshape(group * edge, depth)
        at = pl.multiple_of(g * group * edge, group * edge)
        acc[pl.ds(at, group * edge)] += jnp.dot(lhs, slab_full, preferred_element_type=jnp.float32)
        return carry

    lax.fori_loop(0, PANEL // group, rows, 0)

    @pl.when(step == pl.num_programs(0) - 1)
    def _():
        out[...] = acc[...].astype(out.dtype)


def multiply(info, row_ids, pair_ids, slab_ids, row_all, pair_all, slab_all):
    slots, edge = row_all.shape[1], row_all.shape[2]
    held = (1, slots, edge, edge)
    return pl.pallas_call(
        product_kernel,
        grid_spec=pltpu.PrefetchScalarGridSpec(
            num_scalar_prefetch=4,
            grid=(STEPS,),
            in_specs=[
                pl.BlockSpec(held, lambda s, *_: (s, 0, 0, 0)),
                pl.BlockSpec(held, lambda s, *_: (s, 0, 0, 0)),
                pl.BlockSpec((1,) + slab_all.shape[1:], lambda s, info, *_: (info[8 + s], 0, 0, 0)),
            ],
            out_specs=pl.BlockSpec((PANEL * edge, SLAB * edge), lambda s, *_: (0, 0)),
            scratch_shapes=[
                pltpu.VMEM((PANEL + 1, edge, PANEL * edge), jnp.bfloat16),
                pltpu.VMEM((PANEL + 1, edge, SLAB * edge), jnp.bfloat16),
                pltpu.VMEM((PANEL * edge, SLAB * edge), jnp.float32),
            ],
        ),
        out_shape=jax.ShapeDtypeStruct((PANEL * edge, SLAB * edge), jnp.bfloat16),
        compiler_params=pltpu.CompilerParams(vmem_limit_bytes=50 * 2**20),
    )(info, row_ids, pair_ids, slab_ids, row_all, pair_all, slab_all)


def on_device(stored_blocks, stored_ids, slab_blocks, slab_ids, pair_lists):
    r = lax.axis_index("row")
    c = lax.axis_index("col")
    stride = lax.axis_size("col") // STEPS
    bits = lax.axis_size("row").bit_length() - 1
    ids = jnp.concatenate(
        [
            jnp.pad(stored_ids[0, 0], ((0, 0), (0, 128 - stored_ids.shape[-1]))),
            jnp.pad(slab_ids[0, 0], ((0, 2), (0, 128 - slab_ids.shape[-1]))),
        ]
    )
    row_all, pair_all, slab_all, row_i, pair_i, slab_i = gather(
        stored_blocks[0, 0], slab_blocks[0, 0], ids, stride, bits
    )
    pos = c // stride
    steps = jnp.arange(STEPS, dtype=jnp.int32)
    zero = jnp.zeros((2,), jnp.int32)
    info = jnp.concatenate(
        [jnp.stack([r, c]).astype(jnp.int32), zero, steps * stride + c % stride, steps ^ pos]
    )
    return multiply(info, row_i, pair_i, slab_i, row_all, pair_all, slab_all)


def solution(mesh):
    return jax.shard_map(
        on_device,
        mesh=mesh,
        in_specs=(
            P("row", "col", None, None, None),
            P("row", "col", None, None),
            P("row", "col", None, None, None),
            P("row", "col", None, None),
            P("row", "col", None, None, None),
        ),
        out_specs=P("row", "col"),
        check_vma=False,
    )
```

```python
import functools

import jax
import jax.numpy as jnp
from jax import lax
from jax.experimental import pallas as pl
from jax.experimental.pallas import tpu as pltpu
from jax.sharding import PartitionSpec as P

PANEL = 16
SLAB = 2
STEPS = 4
CHUNKS = 4
MESH = pl.DeviceIdType.MESH


def flipped(value, mask, bits):
    out = value
    for b in range(bits):
        w = 2**b
        out = out + ((mask // w) % 2) * (w - 2 * w * ((value // w) % 2))
    return out


def gather_kernel(
    stride, bits, own, slab, ids, out, blocks, slabs, row_ids, pair_ids, slab_ids,
    stage, dense, right_all, acc, table, scalars,
    z_send, z_recv, p_send, p_recv, b_send, b_recv, l_sem, t_sem,
):
    r = lax.axis_index("row")
    c = lax.axis_index("col")
    pos = c // stride
    rem = c % stride
    left = c - stride
    right = c + stride
    slots, edge = own.shape[0], own.shape[1]
    size = slots // CHUNKS
    slab_slots = slab.shape[0]

    def partner(s):
        return flipped(r, s * stride + rem, bits)

    def shifted(t):
        return flipped(r, t * stride, bits)

    bar = pltpu.get_barrier_semaphore()

    def greet(row, col):
        pl.semaphore_signal(bar, inc=1, device_id=(row, col), device_id_type=MESH)

    def cond_kind(s):
        return s * stride + rem > 0

    @pl.when(pos > 0)
    def _():
        greet(r, left)

    @pl.when(pos < STEPS - 1)
    def _():
        greet(r, right)

    for s in range(STEPS):
        @pl.when(cond_kind(s))
        def _():
            greet(partner(s), c)
    for t in range(1, STEPS):
        greet(shifted(t), c)

    ends = jnp.minimum(pos, 1) + jnp.minimum(STEPS - 1 - pos, 1)
    pl.semaphore_wait(bar, ends + jnp.minimum(rem, 1) + 2 * (STEPS - 1))

    def piece(ref, id_ref, ch):
        return id_ref if ch == 0 else ref.at[pl.ds((ch - 1) * size, size)]

    def landed(s, ch):
        return row_ids.at[s] if ch == 0 else blocks.at[s, pl.ds(1 + (ch - 1) * size, size)]

    def paired(s, ch):
        return pair_ids.at[s] if ch == 0 else blocks.at[s, pl.ds(1 + slots + (ch - 1) * size, size)]

    def along(src, s, ch, way):
        return pltpu.make_async_remote_copy(
            src_ref=src, dst_ref=landed(s, ch), send_sem=z_send.at[way, s, ch],
            recv_sem=z_recv.at[s, ch], device_id=(r, right if way else left), device_id_type=MESH)

    def across(src, s, ch):
        return pltpu.make_async_remote_copy(
            src_ref=src, dst_ref=paired(s, ch), send_sem=p_send.at[s, ch],
            recv_sem=p_recv.at[s, ch], device_id=(partner(s), c), device_id_type=MESH)

    def slab_copy(src, t, to, what):
        dst = slab_ids.at[t] if what == 0 else slabs.at[t, pl.ds(1, slab_slots)]
        return pltpu.make_async_remote_copy(
            src_ref=src, dst_ref=dst, send_sem=b_send.at[t, what],
            recv_sem=b_recv.at[t, what], device_id=(shifted(to), c), device_id_type=MESH)

    pieces = range(CHUNKS + 1)
    for ch in pieces:
        mine = piece(own, ids, ch)

        @pl.when(pos > 0)
        def _():
            along(mine, pos, ch, 0).start()

        @pl.when(pos < STEPS - 1)
        def _():
            along(mine, pos, ch, 1).start()

        @pl.when(cond_kind(pos))
        def _():
            across(mine, pos, ch).start()
        if ch == 0:
            for what, src in ((0, ids), (1, slab)):
                slab_copy(src, 2, 2, what).start()
                slab_copy(src, 1, 1, what).start()
    local = (
        pltpu.make_async_copy(own, blocks.at[pos, pl.ds(1, slots)], l_sem.at[0]),
        pltpu.make_async_copy(ids, row_ids.at[pos], l_sem.at[1]),
        pltpu.make_async_copy(slab, slabs.at[0, pl.ds(1, slab_slots)], l_sem.at[2]),
        pltpu.make_async_copy(ids, slab_ids.at[0], l_sem.at[3]),
    )
    for copy in local:
        copy.start()

    zero_block = jnp.zeros((edge, edge), blocks.dtype)
    stage[0] = zero_block
    for s in range(STEPS):
        slabs[s, 0] = zero_block
    acc[...] = jnp.zeros_like(acc)
    sub = lax.broadcasted_iota(jnp.int32, (PANEL, 128), 0)
    lane = lax.broadcasted_iota(jnp.int32, (PANEL, 128), 1)

    def inverted(at_row, at_col, present, base, rows):
        value = jnp.where(present, lane[:1] + (1 + base), 0)
        hit = jnp.where(at_col == sub, value, 0)
        found = jnp.zeros((PANEL, 128), jnp.int32)
        for a in range(rows):
            most = jnp.max(jnp.where(at_row == a, hit, 0), axis=1, keepdims=True)
            found = jnp.where(lane == a, most, found)
        return found

    def process(s):
        q = partner(s)
        low, high = jnp.minimum(r, q) * PANEL, jnp.maximum(r, q) * PANEL
        t = flipped(s, pos, 2)

        def part(ref, base, turn):
            i, j = ref[s, 0:1] - low, ref[s, 1:2] - high
            keep = ref[s, 2:3] > 0
            return inverted(j if turn else i, i if turn else j, keep, base, PANEL)

        @pl.when(r < q)
        def _():
            table[0:PANEL] = jnp.maximum(part(row_ids, 0, False), part(pair_ids, slots, False))

        @pl.when(r > q)
        def _():
            table[0:PANEL] = jnp.maximum(part(row_ids, 0, True), part(pair_ids, slots, True))

        @pl.when(r == q)
        def _():
            i, j = row_ids[s, 0:1] - low, row_ids[s, 1:2] - high
            keep = row_ids[s, 2:3] > 0
            off = jnp.logical_and(keep, i != j)
            table[0:PANEL] = jnp.maximum(
                inverted(i, j, keep, 0, PANEL), inverted(j, i, off, slots, PANEL))

        table[PANEL:] = inverted(
            slab_ids[t, 4:5] - c * SLAB, slab_ids[t, 3:4] - q * PANEL, slab_ids[t, 5:6] > 0, 0, SLAB)
        fetch = pltpu.make_async_copy(table, scalars, t_sem.at[0])
        fetch.start()
        fetch.wait()

        def slab_row(k, carry):
            for n in range(SLAB):
                right_all[k, :, n * edge : (n + 1) * edge] = slabs[t, scalars[PANEL + k, n]]
            return carry

        lax.fori_loop(0, PANEL, slab_row, 0)

        def hold(to, of, count, turn):
            def some(g, carry):
                for x in range(4):
                    block = blocks[s, of + g * 4 + x]
                    stage[to + g * 4 + x] = block.T if turn else block
                return carry

            lax.fori_loop(0, count // 4, some, 0)

        @pl.when(r < q)
        def _():
            hold(1, 1, 2 * slots, False)

        @pl.when(r > q)
        def _():
            hold(1, 1, 2 * slots, True)

        @pl.when(r == q)
        def _():
            hold(1, 1, slots, False)
            hold(1 + slots, 1, slots, True)

        def fill(i, carry):
            for j in range(PANEL):
                dense[i, :, j * edge : (j + 1) * edge] = stage[scalars[j, i]]
            return carry

        lax.fori_loop(0, PANEL, fill, 0)
        depth = PANEL * edge
        slab_full = right_all[...].reshape(depth, SLAB * edge)
        group = 2

        def product(g, carry):
            lhs = dense[pl.ds(g * group, group)].reshape(group * edge, depth)
            at = pl.multiple_of(g * group * edge, group * edge)
            acc[pl.ds(at, group * edge)] += jnp.dot(
                lhs, slab_full, preferred_element_type=jnp.float32)
            return carry

        lax.fori_loop(0, PANEL // group, product, 0)

    second = 1 + pos % 2
    last = (STEPS - 1) * (1 - pos // 2)
    third = 6 - pos - second - last

    def take(s):
        for ch in pieces:
            @pl.when(cond_kind(s))
            def _():
                across(landed(s, ch), s, ch).wait_recv()
        process(s)

    for d in range(1, STEPS):
        for ch in pieces:
            for way in (1, 0):
                s = pos - d if way else pos + d
                here = s >= 0 if way else s <= STEPS - 1
                more = pos < STEPS - 1 if way else pos > 0

                @pl.when(here)
                def _():
                    along(landed(s, ch), s, ch, way).wait_recv()

                    @pl.when(more)
                    def _():
                        along(landed(s, ch), s, ch, way).start()

                    @pl.when(cond_kind(s))
                    def _():
                        across(landed(s, ch), s, ch).start()
            if d == 1 and ch == 1:
                for what, src in ((0, slab_ids.at[2]), (1, slabs.at[2, pl.ds(1, slab_slots)])):
                    slab_copy(src, 2, 2, what).wait_recv()
                    slab_copy(src, 3, 1, what).start()

        if d == 1:
            for copy in local:
                copy.wait()
            for what, src in ((0, ids), (1, slab)):
                slab_copy(src, 1, 1, what).wait()
                slab_copy(src, 2, 2, what).wait_send()
                slab_copy(src, 3, 1, what).wait()
            take(pos)
        if d == 2:
            take(second)
            take(third)
    take(last)
    out[...] = acc[...].astype(out.dtype)
    for s in range(STEPS):
        for ch in pieces:
            @pl.when(cond_kind(s))
            def _():
                across(landed(s, ch), s, ch).wait_send()

            @pl.when(jnp.logical_and(s <= pos, pos < STEPS - 1))
            def _():
                along(landed(s, ch), s, ch, 1).wait_send()

            @pl.when(jnp.logical_and(s >= pos, pos > 0))
            def _():
                along(landed(s, ch), s, ch, 0).wait_send()


def gather(own, slab, ids, stride, bits):
    any_spec = pl.BlockSpec(memory_space=pl.ANY)
    dma = pltpu.SemaphoreType.DMA
    slots, edge = own.shape[0], own.shape[1]
    tile = (PANEL * edge, SLAB * edge)
    listed = pltpu.VMEM((STEPS,) + ids.shape, ids.dtype)
    return pl.pallas_call(
        functools.partial(gather_kernel, stride, bits),
        out_shape=jax.ShapeDtypeStruct(tile, own.dtype),
        in_specs=[any_spec] * 3,
        out_specs=pl.BlockSpec(memory_space=pltpu.VMEM),
        scratch_shapes=[
            pltpu.VMEM((STEPS, 2 * slots + 1, edge, edge), own.dtype),
            pltpu.VMEM((STEPS, slab.shape[0] + 1, edge, edge), own.dtype),
            listed, listed, listed,
            pltpu.VMEM((2 * slots + 1, edge, edge), own.dtype),
            pltpu.VMEM((PANEL, edge, PANEL * edge), own.dtype),
            pltpu.VMEM((PANEL, edge, SLAB * edge), own.dtype),
            pltpu.VMEM(tile, jnp.float32),
            pltpu.VMEM((2 * PANEL, 128), jnp.int32),
            pltpu.SMEM((2 * PANEL, 128), jnp.int32),
            dma((2, STEPS, CHUNKS + 1)), dma((STEPS, CHUNKS + 1)),
            dma((STEPS, CHUNKS + 1)), dma((STEPS, CHUNKS + 1)),
            dma((STEPS, 2)), dma((STEPS, 2)), dma((4,)), dma((1,)),
        ],
        compiler_params=pltpu.CompilerParams(
            collective_id=0, has_side_effects=True, vmem_limit_bytes=56 * 2**20
        ),
    )(own, slab, ids)


def on_device(stored_blocks, stored_ids, slab_blocks, slab_ids, pair_lists):
    stride = lax.axis_size("col") // STEPS
    bits = lax.axis_size("row").bit_length() - 1
    ids = jnp.concatenate(
        [
            jnp.pad(stored_ids[0, 0], ((0, 0), (0, 128 - stored_ids.shape[-1]))),
            jnp.pad(slab_ids[0, 0], ((0, 2), (0, 128 - slab_ids.shape[-1]))),
        ]
    )
    return gather(stored_blocks[0, 0], slab_blocks[0, 0], ids, stride, bits)


def solution(mesh):
    return jax.shard_map(
        on_device,
        mesh=mesh,
        in_specs=(
            P("row", "col", None, None, None),
            P("row", "col", None, None),
            P("row", "col", None, None, None),
            P("row", "col", None, None),
            P("row", "col", None, None, None),
        ),
        out_specs=P("row", "col"),
        check_vma=False,
    )
```

```python
import functools

import jax
import jax.numpy as jnp
from jax import lax
from jax.experimental import pallas as pl
from jax.experimental.pallas import tpu as pltpu
from jax.sharding import PartitionSpec as P

PANEL = 16
SLAB = 2
STEPS = 4
CHUNKS = 8
MESH = pl.DeviceIdType.MESH


def flipped(value, mask, bits):
    out = value
    for b in range(bits):
        w = 2**b
        out = out + ((mask // w) % 2) * (w - 2 * w * ((value // w) % 2))
    return out


def gather_kernel(
    stride, bits, own, slab, ids, out, blocks, slabs, row_ids, pair_ids, slab_ids,
    stage, dense, right_all, acc, table, scalars,
    z_send, z_recv, p_send, p_recv, b_send, b_recv, l_sem, t_sem,
):
    r = lax.axis_index("row")
    c = lax.axis_index("col")
    pos = c // stride
    rem = c % stride
    left = c - stride
    right = c + stride
    slots, edge = own.shape[0], own.shape[1]
    size = slots // CHUNKS
    slab_slots = slab.shape[0]

    def partner(s):
        return flipped(r, s * stride + rem, bits)

    def shifted(t):
        return flipped(r, t * stride, bits)

    bar = pltpu.get_barrier_semaphore()

    def greet(row, col):
        pl.semaphore_signal(bar, inc=1, device_id=(row, col), device_id_type=MESH)

    def cond_kind(s):
        return s * stride + rem > 0

    @pl.when(pos > 0)
    def _():
        greet(r, left)

    @pl.when(pos < STEPS - 1)
    def _():
        greet(r, right)

    for s in range(STEPS):
        @pl.when(cond_kind(s))
        def _():
            greet(partner(s), c)
    for t in range(1, STEPS):
        greet(shifted(t), c)

    ends = jnp.minimum(pos, 1) + jnp.minimum(STEPS - 1 - pos, 1)
    pl.semaphore_wait(bar, ends + jnp.minimum(rem, 1) + 2 * (STEPS - 1))

    def piece(ref, id_ref, ch):
        return id_ref if ch == 0 else ref.at[pl.ds((ch - 1) * size, size)]

    def landed(s, ch):
        return row_ids.at[s] if ch == 0 else blocks.at[s, pl.ds(1 + (ch - 1) * size, size)]

    def paired(s, ch):
        return pair_ids.at[s] if ch == 0 else blocks.at[s, pl.ds(1 + slots + (ch - 1) * size, size)]

    def along(src, s, ch, way):
        return pltpu.make_async_remote_copy(
            src_ref=src, dst_ref=landed(s, ch), send_sem=z_send.at[way, s, ch],
            recv_sem=z_recv.at[s, ch], device_id=(r, right if way else left), device_id_type=MESH)

    def across(src, s, ch):
        return pltpu.make_async_remote_copy(
            src_ref=src, dst_ref=paired(s, ch), send_sem=p_send.at[s, ch],
            recv_sem=p_recv.at[s, ch], device_id=(partner(s), c), device_id_type=MESH)

    def slab_copy(src, t, to, what):
        dst = slab_ids.at[t] if what == 0 else slabs.at[t, pl.ds(1, slab_slots)]
        return pltpu.make_async_remote_copy(
            src_ref=src, dst_ref=dst, send_sem=b_send.at[t, what],
            recv_sem=b_recv.at[t, what], device_id=(shifted(to), c), device_id_type=MESH)

    pieces = range(CHUNKS + 1)
    kept = 1 + CHUNKS // 2
    for ch in pieces:
        mine = piece(own, ids, ch)

        @pl.when(pos > (1 if ch >= kept else 0))
        def _():
            along(mine, pos, ch, 0).start()

        @pl.when(pos < STEPS - 1)
        def _():
            along(mine, pos, ch, 1).start()

        @pl.when(cond_kind(pos))
        def _():
            across(mine, pos, ch).start()
        if ch == 0:
            for what, src in ((0, ids), (1, slab)):
                slab_copy(src, 2, 2, what).start()
                slab_copy(src, 1, 1, what).start()
    local = (
        pltpu.make_async_copy(own, blocks.at[pos, pl.ds(1, slots)], l_sem.at[0]),
        pltpu.make_async_copy(ids, row_ids.at[pos], l_sem.at[1]),
        pltpu.make_async_copy(slab, slabs.at[0, pl.ds(1, slab_slots)], l_sem.at[2]),
        pltpu.make_async_copy(ids, slab_ids.at[0], l_sem.at[3]),
    )
    for copy in local:
        copy.start()

    zero_block = jnp.zeros((edge, edge), blocks.dtype)
    stage[0] = zero_block
    for s in range(STEPS):
        slabs[s, 0] = zero_block
    acc[...] = jnp.zeros_like(acc)
    sub = lax.broadcasted_iota(jnp.int32, (PANEL, 128), 0)
    lane = lax.broadcasted_iota(jnp.int32, (PANEL, 128), 1)

    def inverted(at_row, at_col, present, base, rows):
        value = jnp.where(present, lane[:1] + (1 + base), 0)
        hit = jnp.where(at_col == sub, value, 0)
        found = jnp.zeros((PANEL, 128), jnp.int32)
        for a in range(rows):
            most = jnp.max(jnp.where(at_row == a, hit, 0), axis=1, keepdims=True)
            found = jnp.where(lane == a, most, found)
        return found

    def process(s):
        q = partner(s)
        low, high = jnp.minimum(r, q) * PANEL, jnp.maximum(r, q) * PANEL
        t = flipped(s, pos, 2)

        def part(ref, base, turn):
            i, j = ref[s, 0:1] - low, ref[s, 1:2] - high
            keep = ref[s, 2:3] > 0
            return inverted(j if turn else i, i if turn else j, keep, base, PANEL)

        @pl.when(r < q)
        def _():
            table[0:PANEL] = jnp.maximum(part(row_ids, 0, False), part(pair_ids, slots, False))

        @pl.when(r > q)
        def _():
            table[0:PANEL] = jnp.maximum(part(row_ids, 0, True), part(pair_ids, slots, True))

        @pl.when(r == q)
        def _():
            i, j = row_ids[s, 0:1] - low, row_ids[s, 1:2] - high
            keep = row_ids[s, 2:3] > 0
            off = jnp.logical_and(keep, i != j)
            table[0:PANEL] = jnp.maximum(
                inverted(i, j, keep, 0, PANEL), inverted(j, i, off, slots, PANEL))

        table[PANEL:] = inverted(
            slab_ids[t, 4:5] - c * SLAB, slab_ids[t, 3:4] - q * PANEL, slab_ids[t, 5:6] > 0, 0, SLAB)
        fetch = pltpu.make_async_copy(table, scalars, t_sem.at[0])
        fetch.start()
        fetch.wait()

        def slab_row(k, carry):
            for n in range(SLAB):
                right_all[k, :, n * edge : (n + 1) * edge] = slabs[t, scalars[PANEL + k, n]]
            return carry

        lax.fori_loop(0, PANEL, slab_row, 0)

        def hold(to, of, count, turn):
            def some(g, carry):
                for x in range(4):
                    block = blocks[s, of + g * 4 + x]
                    stage[to + g * 4 + x] = block.T if turn else block
                return carry

            lax.fori_loop(0, count // 4, some, 0)

        @pl.when(r < q)
        def _():
            hold(1, 1, 2 * slots, False)

        @pl.when(r > q)
        def _():
            hold(1, 1, 2 * slots, True)

        @pl.when(r == q)
        def _():
            hold(1, 1, slots, False)
            hold(1 + slots, 1, slots, True)

        def fill(i, carry):
            for j in range(PANEL):
                dense[i, :, j * edge : (j + 1) * edge] = stage[scalars[j, i]]
            return carry

        lax.fori_loop(0, PANEL, fill, 0)
        depth = PANEL * edge
        slab_full = right_all[...].reshape(depth, SLAB * edge)
        group = 2

        def product(g, carry):
            lhs = dense[pl.ds(g * group, group)].reshape(group * edge, depth)
            at = pl.multiple_of(g * group * edge, group * edge)
            acc[pl.ds(at, group * edge)] += jnp.dot(
                lhs, slab_full, preferred_element_type=jnp.float32)
            return carry

        lax.fori_loop(0, PANEL // group, product, 0)

    second = jnp.where(pos == 2, 1, 2)
    last = jnp.where(pos == 0, 1, jnp.where(pos == 1, 3, 0))
    third = 6 - pos - second - last

    def take(s):
        for ch in pieces:
            @pl.when(cond_kind(s))
            def _():
                across(landed(s, ch), s, ch).wait_recv()
        process(s)

    for d in range(1, STEPS):
        for ch in pieces:
            for way in (1, 0):
                s = pos - d if way else pos + d
                here = s >= 0 if way else s <= STEPS - 1
                if d == 1 and not way and ch >= kept:
                    here = jnp.logical_and(here, pos > 0)
                more = pos < STEPS - 1 if way else pos > 0

                @pl.when(here)
                def _():
                    along(landed(s, ch), s, ch, way).wait_recv()

                    @pl.when(more)
                    def _():
                        along(landed(s, ch), s, ch, way).start()

                    @pl.when(cond_kind(s))
                    def _():
                        across(landed(s, ch), s, ch).start()
            if d == 1 and ch == 1:
                for what, src in ((0, slab_ids.at[2]), (1, slabs.at[2, pl.ds(1, slab_slots)])):
                    slab_copy(src, 2, 2, what).wait_recv()
                    slab_copy(src, 3, 1, what).start()

        if d == 1:
            for copy in local:
                copy.wait()
            for what, src in ((0, ids), (1, slab)):
                slab_copy(src, 1, 1, what).wait()
                slab_copy(src, 2, 2, what).wait_send()
                slab_copy(src, 3, 1, what).wait()
            take(pos)
        if d == 2:
            @pl.when(pos == 1)
            def _():
                for ch in range(kept, CHUNKS + 1):
                    along(piece(own, ids, ch), pos, ch, 0).start()

            take(second)
    take(third)

    @pl.when(pos == 0)
    def _():
        for ch in range(kept, CHUNKS + 1):
            along(landed(1, ch), 1, ch, 0).wait_recv()
            across(landed(1, ch), 1, ch).start()

    take(last)
    out[...] = acc[...].astype(out.dtype)
    for s in range(STEPS):
        for ch in pieces:
            @pl.when(cond_kind(s))
            def _():
                across(landed(s, ch), s, ch).wait_send()

            @pl.when(jnp.logical_and(s <= pos, pos < STEPS - 1))
            def _():
                along(landed(s, ch), s, ch, 1).wait_send()

            @pl.when(jnp.logical_and(s >= pos, pos > 0))
            def _():
                along(landed(s, ch), s, ch, 0).wait_send()


def gather(own, slab, ids, stride, bits):
    any_spec = pl.BlockSpec(memory_space=pl.ANY)
    dma = pltpu.SemaphoreType.DMA
    slots, edge = own.shape[0], own.shape[1]
    tile = (PANEL * edge, SLAB * edge)
    listed = pltpu.VMEM((STEPS,) + ids.shape, ids.dtype)
    return pl.pallas_call(
        functools.partial(gather_kernel, stride, bits),
        out_shape=jax.ShapeDtypeStruct(tile, own.dtype),
        in_specs=[any_spec] * 3,
        out_specs=pl.BlockSpec(memory_space=pltpu.VMEM),
        scratch_shapes=[
            pltpu.VMEM((STEPS, 2 * slots + 1, edge, edge), own.dtype),
            pltpu.VMEM((STEPS, slab.shape[0] + 1, edge, edge), own.dtype),
            listed, listed, listed,
            pltpu.VMEM((2 * slots + 1, edge, edge), own.dtype),
            pltpu.VMEM((PANEL, edge, PANEL * edge), own.dtype),
            pltpu.VMEM((PANEL, edge, SLAB * edge), own.dtype),
            pltpu.VMEM(tile, jnp.float32),
            pltpu.VMEM((2 * PANEL, 128), jnp.int32),
            pltpu.SMEM((2 * PANEL, 128), jnp.int32),
            dma((2, STEPS, CHUNKS + 1)), dma((STEPS, CHUNKS + 1)),
            dma((STEPS, CHUNKS + 1)), dma((STEPS, CHUNKS + 1)),
            dma((STEPS, 2)), dma((STEPS, 2)), dma((4,)), dma((1,)),
        ],
        compiler_params=pltpu.CompilerParams(
            collective_id=0, has_side_effects=True, vmem_limit_bytes=56 * 2**20
        ),
    )(own, slab, ids)


def on_device(stored_blocks, stored_ids, slab_blocks, slab_ids, pair_lists):
    stride = lax.axis_size("col") // STEPS
    bits = lax.axis_size("row").bit_length() - 1
    ids = jnp.concatenate(
        [
            jnp.pad(stored_ids[0, 0], ((0, 0), (0, 128 - stored_ids.shape[-1]))),
            jnp.pad(slab_ids[0, 0], ((0, 2), (0, 128 - slab_ids.shape[-1]))),
        ]
    )
    return gather(stored_blocks[0, 0], slab_blocks[0, 0], ids, stride, bits)


def solution(mesh):
    return jax.shard_map(
        on_device,
        mesh=mesh,
        in_specs=(
            P("row", "col", None, None, None),
            P("row", "col", None, None),
            P("row", "col", None, None, None),
            P("row", "col", None, None),
            P("row", "col", None, None, None),
        ),
        out_specs=P("row", "col"),
        check_vma=False,
    )
```

```python
import functools

import jax
import jax.numpy as jnp
from jax import lax
from jax.experimental import pallas as pl
from jax.experimental.pallas import tpu as pltpu
from jax.sharding import PartitionSpec as P

PANEL = 16
SLAB = 2
STEPS = 4
CHUNKS = 4
MESH = pl.DeviceIdType.MESH


def flipped(value, mask, bits):
    out = value
    for b in range(bits):
        w = 2**b
        out = out + ((mask // w) % 2) * (w - 2 * w * ((value // w) % 2))
    return out


def gather_kernel(
    stride, bits, own, slab, ids, out, blocks, slabs, row_ids, pair_ids, slab_ids,
    stage, dense, right_all, acc, table, scalars,
    z_send, z_recv, p_send, p_recv, b_send, b_recv, l_sem, t_sem,
):
    r = lax.axis_index("row")
    c = lax.axis_index("col")
    pos = c // stride
    rem = c % stride
    left = c - stride
    right = c + stride
    slots, edge = own.shape[0], own.shape[1]
    size = slots // CHUNKS
    slab_slots = slab.shape[0]

    def partner(s):
        return flipped(r, s * stride + rem, bits)

    def shifted(t):
        return flipped(r, t * stride, bits)

    bar = pltpu.get_barrier_semaphore()

    def greet(row, col):
        pl.semaphore_signal(bar, inc=1, device_id=(row, col), device_id_type=MESH)

    def cond_kind(s):
        return s * stride + rem > 0

    @pl.when(pos > 0)
    def _():
        greet(r, left)

    @pl.when(pos < STEPS - 1)
    def _():
        greet(r, right)

    for s in range(STEPS):
        @pl.when(cond_kind(s))
        def _():
            greet(partner(s), c)
    for t in range(1, STEPS):
        greet(shifted(t), c)

    ends = jnp.minimum(pos, 1) + jnp.minimum(STEPS - 1 - pos, 1)
    pl.semaphore_wait(bar, ends + jnp.minimum(rem, 1) + 2 * (STEPS - 1))

    def piece(ref, id_ref, ch):
        return id_ref if ch == 0 else ref.at[pl.ds((ch - 1) * size, size)]

    def landed(s, ch):
        return row_ids.at[s] if ch == 0 else blocks.at[s, pl.ds(1 + (ch - 1) * size, size)]

    def paired(s, ch):
        return pair_ids.at[s] if ch == 0 else blocks.at[s, pl.ds(1 + slots + (ch - 1) * size, size)]

    def along(src, s, ch, way):
        return pltpu.make_async_remote_copy(
            src_ref=src, dst_ref=landed(s, ch), send_sem=z_send.at[way, s, ch],
            recv_sem=z_recv.at[s, ch], device_id=(r, right if way else left), device_id_type=MESH)

    def across(src, s, ch):
        return pltpu.make_async_remote_copy(
            src_ref=src, dst_ref=paired(s, ch), send_sem=p_send.at[s, ch],
            recv_sem=p_recv.at[s, ch], device_id=(partner(s), c), device_id_type=MESH)

    def slab_copy(src, t, to, what):
        dst = slab_ids.at[t] if what == 0 else slabs.at[t, pl.ds(1, slab_slots)]
        return pltpu.make_async_remote_copy(
            src_ref=src, dst_ref=dst, send_sem=b_send.at[t, what],
            recv_sem=b_recv.at[t, what], device_id=(shifted(to), c), device_id_type=MESH)

    pieces = range(CHUNKS + 1)
    kept = 1 + CHUNKS // 2
    for ch in pieces:
        mine = piece(own, ids, ch)

        @pl.when(pos > (1 if ch >= kept else 0))
        def _():
            along(mine, pos, ch, 0).start()

        @pl.when(pos < STEPS - 1)
        def _():
            along(mine, pos, ch, 1).start()

        @pl.when(cond_kind(pos))
        def _():
            across(mine, pos, ch).start()
        if ch == 0:
            for what, src in ((0, ids), (1, slab)):
                slab_copy(src, 2, 2, what).start()
                slab_copy(src, 1, 1, what).start()
    local = (
        pltpu.make_async_copy(own, blocks.at[pos, pl.ds(1, slots)], l_sem.at[0]),
        pltpu.make_async_copy(ids, row_ids.at[pos], l_sem.at[1]),
        pltpu.make_async_copy(slab, slabs.at[0, pl.ds(1, slab_slots)], l_sem.at[2]),
        pltpu.make_async_copy(ids, slab_ids.at[0], l_sem.at[3]),
    )
    for copy in local:
        copy.start()

    zero_block = jnp.zeros((edge, edge), blocks.dtype)
    stage[0] = zero_block
    for s in range(STEPS):
        slabs[s, 0] = zero_block
    acc[...] = jnp.zeros_like(acc)
    sub = lax.broadcasted_iota(jnp.int32, (PANEL, 128), 0)
    lane = lax.broadcasted_iota(jnp.int32, (PANEL, 128), 1)

    def inverted(at_row, at_col, present, base, rows):
        value = jnp.where(present, lane[:1] + (1 + base), 0)
        hit = jnp.where(at_col == sub, value, 0)
        found = jnp.zeros((PANEL, 128), jnp.int32)
        for a in range(rows):
            most = jnp.max(jnp.where(at_row == a, hit, 0), axis=1, keepdims=True)
            found = jnp.where(lane == a, most, found)
        return found

    def process(s):
        q = partner(s)
        low, high = jnp.minimum(r, q) * PANEL, jnp.maximum(r, q) * PANEL
        t = flipped(s, pos, 2)

        def part(ref, base, turn):
            i, j = ref[s, 0:1] - low, ref[s, 1:2] - high
            keep = ref[s, 2:3] > 0
            return inverted(j if turn else i, i if turn else j, keep, base, PANEL)

        @pl.when(r < q)
        def _():
            table[0:PANEL] = jnp.maximum(part(row_ids, 0, False), part(pair_ids, slots, False))

        @pl.when(r > q)
        def _():
            table[0:PANEL] = jnp.maximum(part(row_ids, 0, True), part(pair_ids, slots, True))

        @pl.when(r == q)
        def _():
            i, j = row_ids[s, 0:1] - low, row_ids[s, 1:2] - high
            keep = row_ids[s, 2:3] > 0
            off = jnp.logical_and(keep, i != j)
            table[0:PANEL] = jnp.maximum(
                inverted(i, j, keep, 0, PANEL), inverted(j, i, off, slots, PANEL))

        table[PANEL:] = inverted(
            slab_ids[t, 4:5] - c * SLAB, slab_ids[t, 3:4] - q * PANEL, slab_ids[t, 5:6] > 0, 0, SLAB)
        fetch = pltpu.make_async_copy(table, scalars, t_sem.at[0])
        fetch.start()
        fetch.wait()

        def slab_row(k, carry):
            for n in range(SLAB):
                right_all[k, :, n * edge : (n + 1) * edge] = slabs[t, scalars[PANEL + k, n]]
            return carry

        lax.fori_loop(0, PANEL, slab_row, 0)

        def hold(to, of, count, turn):
            def some(g, carry):
                for x in range(4):
                    block = blocks[s, of + g * 4 + x]
                    stage[to + g * 4 + x] = block.T if turn else block
                return carry

            lax.fori_loop(0, count // 4, some, 0)

        @pl.when(r < q)
        def _():
            hold(1, 1, 2 * slots, False)

        @pl.when(r > q)
        def _():
            hold(1, 1, 2 * slots, True)

        @pl.when(r == q)
        def _():
            hold(1, 1, slots, False)
            hold(1 + slots, 1, slots, True)

        def fill(i, carry):
            for j in range(PANEL):
                dense[i, :, j * edge : (j + 1) * edge] = stage[scalars[j, i]]
            return carry

        lax.fori_loop(0, PANEL, fill, 0)
        depth = PANEL * edge
        slab_full = right_all[...].reshape(depth, SLAB * edge)
        group = 2

        def product(g, carry):
            lhs = dense[pl.ds(g * group, group)].reshape(group * edge, depth)
            at = pl.multiple_of(g * group * edge, group * edge)
            acc[pl.ds(at, group * edge)] += jnp.dot(
                lhs, slab_full, preferred_element_type=jnp.float32)
            return carry

        lax.fori_loop(0, PANEL // group, product, 0)

    second = jnp.where(pos == 2, 1, 2)
    last = jnp.where(pos == 0, 1, jnp.where(pos == 1, 3, 0))
    third = 6 - pos - second - last

    def take(s):
        for ch in pieces:
            @pl.when(cond_kind(s))
            def _():
                across(landed(s, ch), s, ch).wait_recv()
        process(s)

    for d in range(1, STEPS):
        for ch in pieces:
            for way in (1, 0):
                s = pos - d if way else pos + d
                here = s >= 0 if way else s <= STEPS - 1
                if d == 1 and not way and ch >= kept:
                    here = jnp.logical_and(here, pos > 0)
                more = pos < STEPS - 1 if way else pos > 0

                @pl.when(here)
                def _():
                    along(landed(s, ch), s, ch, way).wait_recv()

                    @pl.when(more)
                    def _():
                        along(landed(s, ch), s, ch, way).start()

                    @pl.when(cond_kind(s))
                    def _():
                        across(landed(s, ch), s, ch).start()
            if d == 1 and ch == 1:
                for what, src in ((0, slab_ids.at[2]), (1, slabs.at[2, pl.ds(1, slab_slots)])):
                    slab_copy(src, 2, 2, what).wait_recv()
                    slab_copy(src, 3, 1, what).start()

        if d == 1:
            for copy in local:
                copy.wait()
            for what, src in ((0, ids), (1, slab)):
                slab_copy(src, 1, 1, what).wait()
                slab_copy(src, 2, 2, what).wait_send()
                slab_copy(src, 3, 1, what).wait()
            take(pos)
        if d == 2:
            @pl.when(pos == 1)
            def _():
                for ch in range(kept, CHUNKS + 1):
                    along(piece(own, ids, ch), pos, ch, 0).start()

            take(second)
    take(third)

    @pl.when(pos == 0)
    def _():
        for ch in range(kept, CHUNKS + 1):
            along(landed(1, ch), 1, ch, 0).wait_recv()
            across(landed(1, ch), 1, ch).start()

    take(last)
    out[...] = acc[...].astype(out.dtype)
    for s in range(STEPS):
        for ch in pieces:
            @pl.when(cond_kind(s))
            def _():
                across(landed(s, ch), s, ch).wait_send()

            @pl.when(jnp.logical_and(s <= pos, pos < STEPS - 1))
            def _():
                along(landed(s, ch), s, ch, 1).wait_send()

            @pl.when(jnp.logical_and(s >= pos, pos > 0))
            def _():
                along(landed(s, ch), s, ch, 0).wait_send()


def gather(own, slab, ids, stride, bits):
    any_spec = pl.BlockSpec(memory_space=pl.ANY)
    dma = pltpu.SemaphoreType.DMA
    slots, edge = own.shape[0], own.shape[1]
    tile = (PANEL * edge, SLAB * edge)
    listed = pltpu.VMEM((STEPS,) + ids.shape, ids.dtype)
    return pl.pallas_call(
        functools.partial(gather_kernel, stride, bits),
        out_shape=jax.ShapeDtypeStruct(tile, own.dtype),
        in_specs=[any_spec] * 3,
        out_specs=pl.BlockSpec(memory_space=pltpu.VMEM),
        scratch_shapes=[
            pltpu.VMEM((STEPS, 2 * slots + 1, edge, edge), own.dtype),
            pltpu.VMEM((STEPS, slab.shape[0] + 1, edge, edge), own.dtype),
            listed, listed, listed,
            pltpu.VMEM((2 * slots + 1, edge, edge), own.dtype),
            pltpu.VMEM((PANEL, edge, PANEL * edge), own.dtype),
            pltpu.VMEM((PANEL, edge, SLAB * edge), own.dtype),
            pltpu.VMEM(tile, jnp.float32),
            pltpu.VMEM((2 * PANEL, 128), jnp.int32),
            pltpu.SMEM((2 * PANEL, 128), jnp.int32),
            dma((2, STEPS, CHUNKS + 1)), dma((STEPS, CHUNKS + 1)),
            dma((STEPS, CHUNKS + 1)), dma((STEPS, CHUNKS + 1)),
            dma((STEPS, 2)), dma((STEPS, 2)), dma((4,)), dma((1,)),
        ],
        compiler_params=pltpu.CompilerParams(
            collective_id=0, has_side_effects=True, vmem_limit_bytes=56 * 2**20
        ),
    )(own, slab, ids)


def on_device(stored_blocks, stored_ids, slab_blocks, slab_ids, pair_lists):
    stride = lax.axis_size("col") // STEPS
    bits = lax.axis_size("row").bit_length() - 1
    ids = jnp.concatenate(
        [
            jnp.pad(stored_ids[0, 0], ((0, 0), (0, 128 - stored_ids.shape[-1]))),
            jnp.pad(slab_ids[0, 0], ((0, 2), (0, 128 - slab_ids.shape[-1]))),
        ]
    )
    return gather(stored_blocks[0, 0], slab_blocks[0, 0], ids, stride, bits)


def solution(mesh):
    return jax.shard_map(
        on_device,
        mesh=mesh,
        in_specs=(
            P("row", "col", None, None, None),
            P("row", "col", None, None),
            P("row", "col", None, None, None),
            P("row", "col", None, None),
            P("row", "col", None, None, None),
        ),
        out_specs=P("row", "col"),
        check_vma=False,
    )
```
